128 devices in a mesh: sub: 8 (over z_hi, x), beam: 16 (over z_lo, y, core).
Axes of the slice: x: 4, y: 4, z: 4 (z_hi: 2, z_lo: 2; z = z_hi * 2 + z_lo), core: 2. Of those that a mesh axis runs over, the one named last changes fastest.
Arguments:
- voltages: bfloat16 [1024, 256, 2, 1024], P(('sub', 'beam')), may hold values from -6 to 6
- weights: bfloat16 [256, 2, 1024, 1024], P(('sub', 'beam')), may hold values from -0.1875 to 0.1875
- antenna_map: int32 [1024], replicated, may hold values from 0 to 1023, each once
- delays: int32 [256, 32], P('sub'), may hold values from 0 to 127, as said below
Outputs:
- filterbank: bfloat16 [256, 1024, 256], P('sub', 'beam')
- series: float32 [32, 1024, 128], P('sub', 'beam')
The draws below stay inside these ranges and needn't reach their ends.
Inputs may be any that keep to these rules, and one draw needn't show every extreme that they name: antenna_map is a permutation of the antennas. delays never rise with the channel and never fall with the trial; trial 0 has no delay.
All inputs are finite; a program needn't handle non-finite values.
Results may differ from the reference program's by a relative error of at most 0.008.
Values may be sent and summed in bfloat16 or wider, within the bound.
No kernel may reach another device: no remote copies, remote signals or barrier semaphores. Data moves between devices by JAX's collectives and lax.ppermute only.
A program may use at most 64 MiB of HBM per device.

```python
import math
import jax
import jax.numpy as jnp
from jax import lax

A = 1024
NFFT = 1024
C = 256
B = 1024
TRIALS = 32
MAXD = 128
OUT = 128
FR = 256


def draw_delays(key, part):
    inner = jax.random.randint(key, (TRIALS - 2,), 0, MAXD, dtype=jnp.int32)
    measures = jnp.sort(jnp.concatenate([jnp.zeros((1,), jnp.int32), inner, jnp.full((1,), MAXD - 1, jnp.int32)]))
    channel = jnp.arange(C, dtype=jnp.int32)
    curve = 2 ** 30 // ((C + channel) * (C + channel))
    return measures[None, :] * curve[:, None] // curve[0]


def level_of(key, extent, shards, smallest, largest):
    factor_of = 1.0
    for dim, shards_of in shards:
        heights = jax.random.uniform(jax.random.fold_in(jax.random.fold_in(key, 6), dim), (shards_of,), jnp.float32, smallest / len(shards), largest / len(shards))
        factor_of = factor_of * jnp.repeat(jnp.exp(heights), extent[dim] // shards_of).reshape((-1,) + (1,) * (len(extent) - 1 - dim))
    return factor_of


def gaussian(rng, shape, spread, bound, shards=(), held_as=jnp.bfloat16):
    result = spread * jax.random.normal(rng, shape, jnp.float32)
    if shards:
        result = result * level_of(rng, shape, shards, -0.22, 0.18)
    return jnp.clip(result, -bound, bound).astype(held_as)


def setup_inputs(seed: int = 0) -> dict:
    streams_of = jax.random.split(jax.random.key(seed), 5)
    voltages = gaussian(streams_of[0], (A, FR, 2, NFFT), 1.0, 6.0, ((0, 128),))
    weights = gaussian(streams_of[1], (C, 2, B, A), A ** -0.5, 0.1875, ((0, 128),))
    antenna_map = jax.random.permutation(streams_of[2], A).astype(jnp.int32)
    delays = draw_delays(jax.random.fold_in(streams_of[4], 71), 0)
    return dict(voltages=voltages, weights=weights, antenna_map=antenna_map, delays=delays)


def dft_table():
    sample = jnp.arange(NFFT, dtype=jnp.int32)
    channel = jnp.arange(C, dtype=jnp.int32)
    turns = channel[:, None] * sample[None, :] % NFFT
    phase = turns.astype(jnp.float32) * (2.0 * math.pi / NFFT)
    cosine = jnp.cos(phase) / math.sqrt(NFFT)
    sine = jnp.sin(phase) / math.sqrt(NFFT)
    real_row = jnp.stack([cosine, sine], axis=1)
    imag_row = jnp.stack([-sine, cosine], axis=1)
    return jnp.stack([real_row, imag_row], axis=0).astype(jnp.bfloat16)

def reference(voltages, weights, antenna_map, delays):
    table = dft_table().astype(jnp.float32)

    def channelize(block):
        return jnp.einsum('ocin,afin->aocf', table, block.astype(jnp.float32)).astype(jnp.bfloat16)
    spectra = lax.map(channelize, voltages.reshape(8, A // 8, FR, 2, NFFT)).reshape(A, 2, C, FR)
    by_channel = jnp.transpose(spectra, (2, 0, 1, 3))

    def form_beams(inputs):
        weight_chan, data_chan = inputs
        ordered = jnp.take(weight_chan, antenna_map, axis=2)
        beam_re = jnp.dot(ordered[0], data_chan[:, 0], preferred_element_type=jnp.float32) - jnp.dot(ordered[1], data_chan[:, 1], preferred_element_type=jnp.float32)
        beam_im = jnp.dot(ordered[0], data_chan[:, 1], preferred_element_type=jnp.float32) + jnp.dot(ordered[1], data_chan[:, 0], preferred_element_type=jnp.float32)
        return (beam_re * beam_re + beam_im * beam_im).astype(jnp.bfloat16)
    filterbank = lax.map(form_beams, (weights, by_channel))

    def add_channel(total, inputs):
        power_chan, delay_chan = inputs

        def shifted(delay_value):
            return lax.dynamic_slice_in_dim(power_chan, delay_value, OUT, 1)
        moved = jax.vmap(shifted)(delay_chan).astype(jnp.float32)
        return (total + moved, None)
    start_total = jnp.zeros((TRIALS, B, OUT), jnp.float32)
    total, unused = lax.scan(add_channel, start_total, (filterbank, delays))
    series = total * (1.0 / C)
    return (filterbank, series)
```

```python
import math

import numpy as np
import jax
import jax.numpy as jnp
from jax import lax
from jax.experimental import pallas as pl
from jax.experimental.pallas import tpu as pltpu
from jax.sharding import PartitionSpec as P

A = 1024
NFFT = 1024
C = 256
TRIALS = 32
OUT = 128
FR = 256
HALF = OUT // 2
ROWS = FR - HALF


def dft_table():
    sample = np.arange(NFFT)
    channel = np.arange(C)
    phase = (channel[:, None] * sample[None, :] % NFFT) * (2.0 * math.pi / NFFT)
    cosine = np.cos(phase) / math.sqrt(NFFT)
    sine = np.sin(phase) / math.sqrt(NFFT)
    real_row = np.stack([cosine, sine], axis=1)
    imag_row = np.stack([-sine, cosine], axis=1)
    return np.stack([real_row, imag_row], axis=0).astype(jnp.bfloat16)


def beam_kernel(map_ref, spectra_ref, weight_ref, power_ref, ordered_ref):
    @pl.when(pl.program_id(1) == 0)
    def _():
        rows = lax.broadcasted_iota(jnp.int32, (A, A), 0)
        place = jnp.where(rows == map_ref[...], 1.0, 0.0).astype(jnp.bfloat16)
        for part in range(2):
            piece = spectra_ref[:, part].reshape(A, FR)
            ordered_ref[:, part * FR : (part + 1) * FR] = jnp.dot(
                place, piece, preferred_element_type=jnp.float32
            ).astype(jnp.bfloat16)

    data = ordered_ref[...]
    by_re = jnp.dot(weight_ref[0, 0], data, preferred_element_type=jnp.float32)
    by_im = jnp.dot(weight_ref[0, 1], data, preferred_element_type=jnp.float32)
    beam_re = by_re[:, :FR] - by_im[:, FR:]
    beam_im = by_re[:, FR:] + by_im[:, :FR]
    power = (beam_re * beam_re + beam_im * beam_im).astype(jnp.bfloat16)
    power_ref[...] = power.reshape(power_ref.shape)


def form_beams(antenna_map, spectra, weights, beam_count):
    owned, beams = weights.shape[0], weights.shape[2]
    block = 256
    width = beams // beam_count
    per_block = block // width
    return pl.pallas_call(
        beam_kernel,
        grid=(owned, beams // block),
        in_specs=[
            pl.BlockSpec((1, A), lambda k, b: (0, 0)),
            pl.BlockSpec((spectra.shape[0], 2, spectra.shape[2], FR), lambda k, b: (0, k, 0, 0)),
            pl.BlockSpec((1, 2, block, A), lambda k, b: (k, 0, b, 0)),
        ],
        out_specs=pl.BlockSpec((per_block, 1, width, FR), lambda k, b: (b, k, 0, 0)),
        out_shape=jax.ShapeDtypeStruct((beam_count, owned, width, FR), jnp.bfloat16),
        scratch_shapes=[pltpu.VMEM((A, 2 * FR), jnp.bfloat16)],
        compiler_params=pltpu.CompilerParams(vmem_limit_bytes=32 << 20),
    )(antenna_map.reshape(1, A), spectra, weights)


def dedisperse_kernel(delay_ref, power_ref, out_ref, turned_ref):
    channels = power_ref.shape[0]

    def turn(c, carry):
        power = power_ref[c].astype(jnp.float32)
        both = jnp.concatenate([power, pltpu.roll(power, FR - HALF, 1)], axis=0)
        turned_ref[pl.ds(pl.multiple_of(c * ROWS, 8), ROWS), :] = both.T[:ROWS]
        return carry

    lax.fori_loop(0, channels, turn, 0)

    def trial(t, carry):
        total = turned_ref[pl.ds(delay_ref[0, t], HALF), :]
        for c in range(1, channels):
            total = total + turned_ref[pl.ds(c * ROWS + delay_ref[c, t], HALF), :]
        out_ref[t] = (total * (1.0 / C)).astype(jnp.bfloat16)
        return carry

    lax.fori_loop(0, TRIALS, trial, 0)


def dedisperse(filterbank, delays):
    channels, beams = filterbank.shape[:2]
    return pl.pallas_call(
        dedisperse_kernel,
        in_specs=[
            pl.BlockSpec(memory_space=pltpu.SMEM),
            pl.BlockSpec(memory_space=pltpu.VMEM),
        ],
        out_specs=pl.BlockSpec(memory_space=pltpu.VMEM),
        out_shape=jax.ShapeDtypeStruct((TRIALS, HALF, 2 * beams), jnp.bfloat16),
        scratch_shapes=[pltpu.VMEM((channels * ROWS, 2 * beams), jnp.float32)],
        compiler_params=pltpu.CompilerParams(vmem_limit_bytes=32 << 20),
    )(delays, filterbank)


def sum_kernel(pieces_ref, out_ref):
    beams = out_ref.shape[1]
    for t in range(out_ref.shape[0]):
        total = pieces_ref[0, t].astype(jnp.float32)
        for s in range(1, pieces_ref.shape[0]):
            total = total + pieces_ref[s, t].astype(jnp.float32)
        turned = total.T
        out_ref[t] = jnp.concatenate([turned[:beams], turned[beams:]], axis=1)


def sum_pieces(pieces):
    beams = pieces.shape[3] // 2
    return pl.pallas_call(
        sum_kernel,
        out_shape=jax.ShapeDtypeStruct((pieces.shape[1], beams, OUT), jnp.float32),
    )(pieces)


def on_device(voltages, weights, antenna_map, delays):
    antennas = voltages.shape[0]
    subband_count = lax.axis_size("sub")
    beam_count = lax.axis_size("beam")
    devices = subband_count * beam_count
    owned = C // devices
    table = jnp.asarray(dft_table()).reshape(2, devices, owned, 2, NFFT)
    spectra = jnp.einsum(
        "odkin,afin->dkoaf", table, voltages, preferred_element_type=jnp.float32
    ).astype(jnp.bfloat16)
    spectra = spectra.reshape(devices, owned * 2, antennas, FR)
    moved = lax.all_to_all(spectra, ("sub", "beam"), 0, 0, tiled=True)
    power = form_beams(antenna_map, moved, weights, beam_count)
    filterbank = lax.all_to_all(power, "beam", 0, 0, tiled=True)
    filterbank = filterbank.reshape(beam_count * owned, -1, FR)
    partial = dedisperse(filterbank, delays)
    pieces = partial.reshape(subband_count, TRIALS // subband_count, *partial.shape[1:])
    series = sum_pieces(lax.all_to_all(pieces, "sub", 0, 0, tiled=True))
    return (filterbank, series)


def solution(mesh):
    placed = (
        P(("sub", "beam"), None, None, None),
        P(("sub", "beam"), None, None, None),
        P(),
        P("sub", None),
    )
    return jax.shard_map(
        on_device,
        mesh=mesh,
        in_specs=placed,
        out_specs=(P("sub", "beam", None), P("sub", "beam", None)),
        check_vma=False,
    )
```

```python
import math

import numpy as np
import jax
import jax.numpy as jnp
from jax import lax
from jax.experimental import pallas as pl
from jax.experimental.pallas import tpu as pltpu
from jax.sharding import PartitionSpec as P

A = 1024
NFFT = 1024
C = 256
TRIALS = 32
OUT = 128
FR = 256
HALF = OUT // 2
ROWS = FR - HALF


def dft_table():
    sample = np.arange(NFFT // 4)
    channel = np.arange(C)
    phase = (channel[:, None] * sample[None, :] % NFFT) * (2.0 * math.pi / NFFT)
    cosine = np.cos(phase) / math.sqrt(NFFT)
    sine = np.sin(phase) / math.sqrt(NFFT)
    real_row = np.concatenate([cosine, sine], axis=1)
    imag_row = np.concatenate([-sine, cosine], axis=1)
    rows = np.stack([real_row, imag_row], axis=0)
    rows = rows.reshape(2, C // 4, 4, NFFT // 2).transpose(2, 0, 1, 3)
    return rows.reshape(4, C // 2, NFFT // 2).astype(jnp.bfloat16)


PITCH = 20
SPAN = 65
FRAMES = 16
PAIR = 2


def mix_frames(sample_ref, wide_ref, mixed_ref, row, first):
    for f in range(FRAMES):
        start = row + (first + f) * 16
        wide_ref[PITCH * (first + f) : PITCH * (first + f) + 16, :] = sample_ref[start : start + 16, :].astype(jnp.float32)

    def pick(block, part):
        return wide_ref[pl.ds(PITCH * first + 2 * block + part, FRAMES, stride=PITCH), :]

    for half in range(2):
        re = [pick(2 * j + half, 0) for j in range(4)]
        im = [pick(2 * j + half, 1) for j in range(4)]
        add_re, sub_re = re[0] + re[2], re[0] - re[2]
        add_im, sub_im = im[0] + im[2], im[0] - im[2]
        odd_add_re, odd_sub_re = re[1] + re[3], re[1] - re[3]
        odd_add_im, odd_sub_im = im[1] + im[3], im[1] - im[3]
        mixed = (
            (add_re + odd_add_re, add_im + odd_add_im),
            (sub_re + odd_sub_im, sub_im - odd_sub_re),
            (add_re - odd_add_re, add_im - odd_add_im),
            (sub_re - odd_sub_im, sub_im + odd_sub_re),
        )
        for r in range(4):
            for part in range(2):
                lane = part * 256 + half * 128
                mixed_ref[r, first : first + FRAMES, lane : lane + 128] = mixed[r][part].astype(jnp.bfloat16)


def transform(table_ref, mixed_ref, done_ref, antenna):
    groups = C // 4
    for r in range(4):
        got = lax.dot_general(
            table_ref[r],
            mixed_ref[r],
            (((1,), (1,)), ((), ())),
            preferred_element_type=jnp.float32,
        )
        for part in range(2):
            start = r * 16 + part * 8 + antenna
            for side in range(2):
                done_ref[side, pl.ds(start, groups, stride=SPAN), :] = got[
                    part * groups : part * groups + groups, side * 128 : side * 128 + 128
                ]


def channel_kernel(table_ref, sample_ref, out_ref, wide_a, wide_b, mixed_a, mixed_b, done_ref):
    antenna = pl.program_id(0) * PAIR
    last = PAIR * (pl.num_programs(0) - 1)
    before = jnp.where(antenna == 0, last + 1, antenna - 1)

    @pl.when(antenna == 0)
    def _():
        mixed_b[...] = jnp.zeros(mixed_b.shape, mixed_b.dtype)

    transform(table_ref, mixed_b, done_ref, before)
    for first in range(0, FR, FRAMES):
        mix_frames(sample_ref, wide_a, mixed_a, 0, first)
    transform(table_ref, mixed_a, done_ref, antenna)
    for first in range(0, FR, FRAMES):
        mix_frames(sample_ref, wide_b, mixed_b, FR * 16, first)

    @pl.when(antenna == last)
    def _():
        transform(table_ref, mixed_b, done_ref, antenna + 1)
        for side in range(2):
            lanes = slice(side * 128, side * 128 + 128)
            for q in range(C // 4):
                block = done_ref[side, SPAN * q : SPAN * q + 64, :]
                out_ref[8 * q : 8 * q + 8, :, lanes] = block.reshape(8, 8, 128).astype(jnp.bfloat16)


def channelize(voltages):
    antennas = voltages.shape[0]
    rows = FR * 16
    flat = voltages.reshape(antennas, FR, 2, 8, 128).transpose(0, 1, 3, 2, 4).reshape(antennas * rows, 128)
    flat = pltpu.with_memory_space_constraint(flat, pltpu.HBM)
    table = jnp.asarray(dft_table())
    mixed = pltpu.VMEM((4, FR, NFFT // 2), jnp.bfloat16)
    wide = pltpu.VMEM((FR * PITCH, 128), jnp.float32)
    return pl.pallas_call(
        channel_kernel,
        grid=(antennas // PAIR,),
        in_specs=[
            pl.BlockSpec(table.shape, lambda a: (0, 0, 0)),
            pl.BlockSpec((PAIR * rows, 128), lambda a: (a, 0)),
        ],
        out_specs=pl.BlockSpec((2 * C, antennas, FR), lambda a: (0, 0, 0)),
        out_shape=pltpu.HBM((2 * C, antennas, FR), jnp.bfloat16),
        scratch_shapes=[wide, wide, mixed, mixed, pltpu.VMEM((2, C // 4 * SPAN, 128), jnp.float32)],
        compiler_params=pltpu.CompilerParams(vmem_limit_bytes=32 << 20),
    )(table, flat)


def beam_kernel(spectra_ref, weight_ref, power_ref, data_ref):
    @pl.when(pl.program_id(1) == 0)
    def _():
        for part in range(2):
            data_ref[:, part * FR : (part + 1) * FR] = spectra_ref[:, part].reshape(A, FR)

    block = 256
    width = power_ref.shape[2]
    for first in range(0, weight_ref.shape[2], block):
        both = weight_ref[0, :, first : first + block].reshape(2 * block, A)
        made = jnp.dot(both, data_ref[...], preferred_element_type=jnp.float32)
        beam_re = made[:block, :FR] - made[block:, FR:]
        beam_im = made[:block, FR:] + made[block:, :FR]
        power = (beam_re * beam_re + beam_im * beam_im).astype(jnp.bfloat16)
        power_ref[first // width : (first + block) // width, 0] = power.reshape(block // width, width, FR)


def order_kernel(map_ref, weight_ref, out_ref, place_ref):
    @pl.when((pl.program_id(0) == 0) & (pl.program_id(1) == 0))
    def _():
        rows = lax.broadcasted_iota(jnp.int32, (A, A), 0)
        place_ref[...] = jnp.where(rows == map_ref[...], 1.0, 0.0).astype(jnp.bfloat16)

    both = weight_ref[0].reshape(-1, A)
    moved = jnp.dot(both, place_ref[...], preferred_element_type=jnp.float32)
    out_ref[0] = moved.astype(jnp.bfloat16).reshape(out_ref.shape[1:])


def order_weights(antenna_map, weights):
    owned, beams = weights.shape[0], weights.shape[2]
    block = 256
    spec = pl.BlockSpec((1, 2, block, A), lambda k, b: (k, 0, b, 0))
    return pl.pallas_call(
        order_kernel,
        grid=(owned, beams // block),
        in_specs=[pl.BlockSpec((1, A), lambda k, b: (0, 0)), spec],
        out_specs=spec,
        out_shape=pltpu.HBM(weights.shape, jnp.bfloat16),
        scratch_shapes=[pltpu.VMEM((A, A), jnp.bfloat16)],
        compiler_params=pltpu.CompilerParams(vmem_limit_bytes=16 << 20),
    )(antenna_map.reshape(1, A), pltpu.with_memory_space_constraint(weights, pltpu.HBM))


def form_beams(spectra, weights, beam_count):
    owned, beams = weights.shape[0], weights.shape[2]
    block = 1024
    width = beams // beam_count
    per_block = block // width
    return pl.pallas_call(
        beam_kernel,
        grid=(owned, beams // block),
        in_specs=[
            pl.BlockSpec((spectra.shape[0], 2, spectra.shape[2], FR), lambda k, b: (0, k, 0, 0)),
            pl.BlockSpec((1, 2, block, A), lambda k, b: (k, 0, b, 0)),
        ],
        out_specs=pl.BlockSpec((per_block, 1, width, FR), lambda k, b: (b, k, 0, 0)),
        out_shape=jax.ShapeDtypeStruct((beam_count, owned, width, FR), jnp.bfloat16),
        scratch_shapes=[pltpu.VMEM((A, 2 * FR), jnp.bfloat16)],
        compiler_params=pltpu.CompilerParams(vmem_limit_bytes=32 << 20),
    )(spectra, pltpu.with_memory_space_constraint(weights, pltpu.HBM))


def dedisperse_kernel(delay_ref, power_ref, out_ref, kept_ref, turned_ref, sem):
    channels, beams = power_ref.shape[:2]
    keep = pltpu.make_async_copy(power_ref, kept_ref, sem)
    keep.start()
    rows = lax.broadcasted_iota(jnp.int32, (ROWS, FR), 0)
    lanes = lax.broadcasted_iota(jnp.int32, (ROWS, FR), 1)
    unit = jnp.where(rows == lanes, 1.0, 0.0).astype(jnp.bfloat16)

    for pair in range(channels // 2):
        parts = []
        for c in range(2):
            power = power_ref[2 * pair + c]
            parts += [power, jnp.concatenate([power[:, HALF:], power[:, :HALF]], axis=1)]
        both = lax.dot_general(
            unit,
            jnp.concatenate(parts, axis=0),
            (((1,), (1,)), ((), ())),
            preferred_element_type=jnp.float32,
        )
        for c in range(2):
            start = (2 * pair + c) * ROWS
            turned_ref[start : start + ROWS, :] = both[:, c * 2 * beams : (c + 1) * 2 * beams]

    def trial(pair, carry):
        for t in (2 * pair, 2 * pair + 1):
            total = turned_ref[pl.ds(delay_ref[0, t], HALF), :]
            for c in range(1, channels):
                total = total + turned_ref[pl.ds(c * ROWS + delay_ref[c, t], HALF), :]
            out_ref[t] = (total * (1.0 / C)).astype(jnp.bfloat16)
        return carry

    lax.fori_loop(0, TRIALS // 2, trial, 0)
    keep.wait()


def dedisperse(filterbank, delays):
    channels, beams = filterbank.shape[:2]
    return pl.pallas_call(
        dedisperse_kernel,
        in_specs=[
            pl.BlockSpec(memory_space=pltpu.SMEM),
            pl.BlockSpec(memory_space=pltpu.VMEM),
        ],
        out_specs=(
            pl.BlockSpec(memory_space=pltpu.VMEM),
            pl.BlockSpec(memory_space=pltpu.HBM),
        ),
        out_shape=(
            jax.ShapeDtypeStruct((TRIALS, HALF, 2 * beams), jnp.bfloat16),
            jax.ShapeDtypeStruct(filterbank.shape, filterbank.dtype),
        ),
        scratch_shapes=[
            pltpu.VMEM((channels * ROWS, 2 * beams), jnp.float32),
            pltpu.SemaphoreType.DMA,
        ],
        compiler_params=pltpu.CompilerParams(vmem_limit_bytes=16 << 20),
    )(delays, filterbank)


def sum_kernel(pieces_ref, out_ref):
    beams = out_ref.shape[1]
    for t in range(out_ref.shape[0]):
        total = pieces_ref[0, t].astype(jnp.float32)
        for s in range(1, pieces_ref.shape[0]):
            total = total + pieces_ref[s, t].astype(jnp.float32)
        turned = total.T
        out_ref[t] = jnp.concatenate([turned[:beams], turned[beams:]], axis=1)


def sum_pieces(pieces):
    beams = pieces.shape[3] // 2
    return pl.pallas_call(
        sum_kernel,
        out_shape=jax.ShapeDtypeStruct((pieces.shape[1], beams, OUT), jnp.float32),
    )(pieces)


def on_device(voltages, weights, antenna_map, delays):
    subband_count = lax.axis_size("sub")
    beam_count = lax.axis_size("beam")
    devices = subband_count * beam_count
    owned = C // devices
    spectra = channelize(voltages)
    spectra = spectra.reshape(devices, owned * 2, voltages.shape[0], FR)
    moved = lax.all_to_all(spectra, ("sub", "beam"), 0, 0, tiled=True)
    ordered = order_weights(antenna_map, weights)
    power = form_beams(moved, ordered, beam_count)
    filterbank = lax.all_to_all(power, "beam", 0, 0, tiled=True)
    filterbank = filterbank.reshape(beam_count * owned, -1, FR)
    partial, filterbank = dedisperse(filterbank, delays)
    pieces = partial.reshape(subband_count, TRIALS // subband_count, *partial.shape[1:])
    series = sum_pieces(lax.all_to_all(pieces, "sub", 0, 0, tiled=True))
    return (filterbank, series)


def solution(mesh):
    placed = (
        P(("sub", "beam"), None, None, None),
        P(("sub", "beam"), None, None, None),
        P(),
        P("sub", None),
    )
    return jax.shard_map(
        on_device,
        mesh=mesh,
        in_specs=placed,
        out_specs=(P("sub", "beam", None), P("sub", "beam", None)),
        check_vma=False,
    )
```

```python
import math

import numpy as np
import jax
import jax.numpy as jnp
from jax import lax
from jax.experimental import pallas as pl
from jax.experimental.pallas import tpu as pltpu
from jax.sharding import Mesh, PartitionSpec as P

A = 1024
NFFT = 1024
C = 256
TRIALS = 32
OUT = 128
FR = 256
HALF = OUT // 2
AXES = (("zh", 2), ("x", 4), ("zl", 2), ("y", 4), ("core", 2))
EVERY = tuple(name for name, size in AXES)
SIZES = tuple(size for name, size in AXES)
ORDER = ("core", "x", "y", "zh", "zl")
TURN = tuple(EVERY.index(name) for name in ORDER)
ROWS = FR - HALF


def dft_table():
    sample = np.arange(NFFT // 4)
    channel = np.arange(C)
    phase = (channel[:, None] * sample[None, :] % NFFT) * (2.0 * math.pi / NFFT)
    cosine = np.cos(phase) / math.sqrt(NFFT)
    sine = np.sin(phase) / math.sqrt(NFFT)
    real_row = np.concatenate([cosine, sine], axis=1)
    imag_row = np.concatenate([-sine, cosine], axis=1)
    rows = np.stack([real_row, imag_row], axis=0)
    rows = rows.reshape(2, C // 4, 4, NFFT // 2).transpose(2, 0, 1, 3)
    return rows.reshape(4, C // 2, NFFT // 2).astype(jnp.bfloat16)


PLACE = np.argsort(np.arange(C // 2).reshape(SIZES).transpose(TURN).reshape(-1)).tolist()
PITCH = 20
SPAN = 65
FRAMES = 16
PAIR = 2


def mix_frames(sample_ref, wide_ref, mixed_ref, row, first):
    for f in range(FRAMES):
        start = row + (first + f) * 16
        wide_ref[PITCH * (first + f) : PITCH * (first + f) + 16, :] = sample_ref[start : start + 16, :].astype(jnp.float32)

    def pick(block, part):
        return wide_ref[pl.ds(PITCH * first + 2 * block + part, FRAMES, stride=PITCH), :]

    for half in range(2):
        re = [pick(2 * j + half, 0) for j in range(4)]
        im = [pick(2 * j + half, 1) for j in range(4)]
        add_re, sub_re = re[0] + re[2], re[0] - re[2]
        add_im, sub_im = im[0] + im[2], im[0] - im[2]
        odd_add_re, odd_sub_re = re[1] + re[3], re[1] - re[3]
        odd_add_im, odd_sub_im = im[1] + im[3], im[1] - im[3]
        mixed = (
            (add_re + odd_add_re, add_im + odd_add_im),
            (sub_re + odd_sub_im, sub_im - odd_sub_re),
            (add_re - odd_add_re, add_im - odd_add_im),
            (sub_re - odd_sub_im, sub_im + odd_sub_re),
        )
        for r in range(4):
            for part in range(2):
                lane = part * 256 + half * 128
                mixed_ref[r, first : first + FRAMES, lane : lane + 128] = mixed[r][part].astype(jnp.bfloat16)


def transform(table_ref, mixed_ref, done_ref, antenna):
    groups = C // 4
    for r in range(4):
        got = lax.dot_general(
            table_ref[r],
            mixed_ref[r],
            (((1,), (1,)), ((), ())),
            preferred_element_type=jnp.float32,
        )
        for part in range(2):
            start = r * 16 + part * 8 + antenna
            for side in range(2):
                done_ref[side, pl.ds(start, groups, stride=SPAN), :] = got[
                    part * groups : part * groups + groups, side * 128 : side * 128 + 128
                ]


def channel_kernel(table_ref, sample_ref, out_ref, wide_a, wide_b, mixed_a, mixed_b, done_ref):
    antenna = pl.program_id(0) * PAIR
    last = PAIR * (pl.num_programs(0) - 1)
    before = jnp.where(antenna == 0, last + 1, antenna - 1)

    @pl.when(antenna == 0)
    def _():
        mixed_b[...] = jnp.zeros(mixed_b.shape, mixed_b.dtype)

    transform(table_ref, mixed_b, done_ref, before)
    for first in range(0, FR, FRAMES):
        mix_frames(sample_ref, wide_a, mixed_a, 0, first)
    transform(table_ref, mixed_a, done_ref, antenna)
    for first in range(0, FR, FRAMES):
        mix_frames(sample_ref, wide_b, mixed_b, FR * 16, first)

    @pl.when(antenna == last)
    def _():
        transform(table_ref, mixed_b, done_ref, antenna + 1)
        for side in range(2):
            lanes = slice(side * 128, side * 128 + 128)
            for q in range(C // 4):
                block = done_ref[side, SPAN * q : SPAN * q + 64, :].reshape(8, 8, 128).astype(jnp.bfloat16)
                for core in range(2):
                    start = 4 * PLACE[2 * q + core]
                    out_ref[start : start + 4, :, lanes] = block[4 * core : 4 * core + 4]


def channelize(voltages):
    antennas = voltages.shape[0]
    rows = FR * 16
    flat = voltages.reshape(antennas, FR, 2, 8, 128).transpose(0, 1, 3, 2, 4).reshape(antennas * rows, 128)
    flat = pltpu.with_memory_space_constraint(flat, pltpu.HBM)
    table = pltpu.with_memory_space_constraint(jnp.asarray(dft_table()), pltpu.HBM)
    mixed = pltpu.VMEM((4, FR, NFFT // 2), jnp.bfloat16)
    wide = pltpu.VMEM((FR * PITCH, 128), jnp.float32)
    return pl.pallas_call(
        channel_kernel,
        grid=(antennas // PAIR,),
        in_specs=[
            pl.BlockSpec(table.shape, lambda a: (0, 0, 0)),
            pl.BlockSpec((PAIR * rows, 128), lambda a: (a, 0)),
        ],
        out_specs=pl.BlockSpec((2 * C, antennas, FR), lambda a: (0, 0, 0)),
        out_shape=pltpu.HBM((2 * C, antennas, FR), jnp.bfloat16),
        scratch_shapes=[wide, wide, mixed, mixed, pltpu.VMEM((2, C // 4 * SPAN, 128), jnp.float32)],
        compiler_params=pltpu.CompilerParams(vmem_limit_bytes=32 << 20),
    )(table, flat)


def beam_kernel(spectra_ref, weight_ref, power_ref, data_ref):
    @pl.when(pl.program_id(1) == 0)
    def _():
        for part in range(2):
            data_ref[:, part * FR : (part + 1) * FR] = spectra_ref[:, part].reshape(A, FR)

    block = 256
    width = power_ref.shape[2]
    for first in range(0, weight_ref.shape[2], block):
        both = weight_ref[0, :, first : first + block].reshape(2 * block, A)
        made = jnp.dot(both, data_ref[...], preferred_element_type=jnp.float32)
        beam_re = made[:block, :FR] - made[block:, FR:]
        beam_im = made[:block, FR:] + made[block:, :FR]
        power = (beam_re * beam_re + beam_im * beam_im).astype(jnp.bfloat16)
        power_ref[first // width : (first + block) // width, 0] = power.reshape(block // width, width, FR)


def order_kernel(map_ref, weight_ref, out_ref, place_ref):
    @pl.when((pl.program_id(0) == 0) & (pl.program_id(1) == 0))
    def _():
        rows = lax.broadcasted_iota(jnp.int32, (A, A), 0)
        place_ref[...] = jnp.where(rows == map_ref[...], 1.0, 0.0).astype(jnp.bfloat16)

    both = weight_ref[0].reshape(-1, A)
    moved = jnp.dot(both, place_ref[...], preferred_element_type=jnp.float32)
    out_ref[0] = moved.astype(jnp.bfloat16).reshape(out_ref.shape[1:])


def order_weights(antenna_map, weights):
    owned, beams = weights.shape[0], weights.shape[2]
    block = 256
    spec = pl.BlockSpec((1, 2, block, A), lambda k, b: (k, 0, b, 0))
    return pl.pallas_call(
        order_kernel,
        grid=(owned, beams // block),
        in_specs=[pl.BlockSpec((1, A), lambda k, b: (0, 0)), spec],
        out_specs=spec,
        out_shape=pltpu.HBM(weights.shape, jnp.bfloat16),
        scratch_shapes=[pltpu.VMEM((A, A), jnp.bfloat16)],
        compiler_params=pltpu.CompilerParams(vmem_limit_bytes=16 << 20),
    )(antenna_map.reshape(1, A), pltpu.with_memory_space_constraint(weights, pltpu.HBM))


def form_beams(spectra, weights, beam_count):
    owned, beams = weights.shape[0], weights.shape[2]
    block = 1024
    width = beams // beam_count
    per_block = block // width
    return pl.pallas_call(
        beam_kernel,
        grid=(owned, beams // block),
        in_specs=[
            pl.BlockSpec((spectra.shape[0], 2, spectra.shape[2], FR), lambda k, b: (0, k, 0, 0)),
            pl.BlockSpec((1, 2, block, A), lambda k, b: (k, 0, b, 0)),
        ],
        out_specs=pl.BlockSpec((per_block, 1, width, FR), lambda k, b: (b, k, 0, 0)),
        out_shape=jax.ShapeDtypeStruct((beam_count, owned, width, FR), jnp.bfloat16),
        scratch_shapes=[pltpu.VMEM((A, 2 * FR), jnp.bfloat16)],
        compiler_params=pltpu.CompilerParams(vmem_limit_bytes=32 << 20),
    )(spectra, pltpu.with_memory_space_constraint(weights, pltpu.HBM))


def dedisperse_kernel(delay_ref, core_ref, near_ref, far_ref, out_ref, kept_ref, turned_ref, sems):
    chips, _, owned, beams = near_ref.shape[:4]
    channels = chips * 2 * owned
    core = core_ref[0]
    copies = [
        pltpu.make_async_copy(near_ref.at[:, core], kept_ref.at[:, core], sems.at[0]),
        pltpu.make_async_copy(far_ref, kept_ref.at[:, 1 - core], sems.at[1]),
    ]
    for copy in copies:
        copy.start()
    rows = lax.broadcasted_iota(jnp.int32, (ROWS, FR), 0)
    lanes = lax.broadcasted_iota(jnp.int32, (ROWS, FR), 1)
    unit = jnp.where(rows == lanes, 1.0, 0.0).astype(jnp.bfloat16)

    for chip in range(chips):
        for side in range(2):
            parts = []
            for k in range(owned):
                power = near_ref[chip, core, k] if side == 0 else far_ref[chip, k]
                parts += [power, jnp.concatenate([power[:, HALF:], power[:, :HALF]], axis=1)]
            both = lax.dot_general(
                unit,
                jnp.concatenate(parts, axis=0),
                (((1,), (1,)), ((), ())),
                preferred_element_type=jnp.float32,
            )
            source = core if side == 0 else 1 - core
            for k in range(owned):
                start = pl.multiple_of(((chip * 2 + source) * owned + k) * ROWS, 8)
                turned_ref[pl.ds(start, ROWS), :] = both[:, k * 2 * beams : (k + 1) * 2 * beams]

    def trial(pair, carry):
        for t in (2 * pair, 2 * pair + 1):
            total = turned_ref[pl.ds(delay_ref[0, t], HALF), :]
            for c in range(1, channels):
                total = total + turned_ref[pl.ds(c * ROWS + delay_ref[c, t], HALF), :]
            out_ref[t] = (total * (1.0 / C)).astype(jnp.bfloat16)
        return carry

    lax.fori_loop(0, TRIALS // 2, trial, 0)
    for copy in copies:
        copy.wait()


def dedisperse(delays, core, near, far):
    chips, _, owned, beams = near.shape[:4]
    channels = chips * 2 * owned
    return pl.pallas_call(
        dedisperse_kernel,
        in_specs=[
            pl.BlockSpec(memory_space=pltpu.SMEM),
            pl.BlockSpec(memory_space=pltpu.SMEM),
            pl.BlockSpec(memory_space=pltpu.VMEM),
            pl.BlockSpec(memory_space=pltpu.VMEM),
        ],
        out_specs=(
            pl.BlockSpec(memory_space=pltpu.VMEM),
            pl.BlockSpec(memory_space=pltpu.HBM),
        ),
        out_shape=(
            jax.ShapeDtypeStruct((TRIALS, HALF, 2 * beams), jnp.bfloat16),
            jax.ShapeDtypeStruct(near.shape, near.dtype),
        ),
        scratch_shapes=[
            pltpu.VMEM((channels * ROWS, 2 * beams), jnp.float32),
            pltpu.SemaphoreType.DMA((2,)),
        ],
        compiler_params=pltpu.CompilerParams(vmem_limit_bytes=16 << 20),
    )(delays, core.reshape(1), near, far)


def sum_kernel(pieces_ref, out_ref):
    beams = out_ref.shape[1]
    for t in range(out_ref.shape[0]):
        total = pieces_ref[0, t].astype(jnp.float32)
        for s in range(1, pieces_ref.shape[0]):
            total = total + pieces_ref[s, t].astype(jnp.float32)
        turned = total.T
        out_ref[t] = jnp.concatenate([turned[:beams], turned[beams:]], axis=1)


def sum_pieces(pieces):
    beams = pieces.shape[3] // 2
    return pl.pallas_call(
        sum_kernel,
        out_shape=jax.ShapeDtypeStruct((pieces.shape[1], beams, OUT), jnp.float32),
    )(pieces)


def on_device(voltages, weights, antenna_map, delays):
    sub, beam = EVERY[:2], EVERY[2:]
    subband_count, beam_count = lax.axis_size(sub), lax.axis_size(beam)
    owned = weights.shape[0]
    core = lax.axis_index("core")
    spectra = channelize(voltages)
    spectra = spectra.reshape(-1, owned * 2, voltages.shape[0], FR)
    moved = lax.all_to_all(spectra, ORDER, 0, 0, tiled=True)
    arrived = antenna_map.reshape(*SIZES, -1).transpose(*TURN, len(SIZES)).reshape(A)
    ordered = order_weights(arrived, weights)
    power = form_beams(moved, ordered, beam_count)
    power = power.reshape(beam_count // 2, 2, *power.shape[1:])
    near = lax.all_to_all(power, ("zl", "y"), 0, 0, tiled=True)
    away = lax.dynamic_index_in_dim(near, 1 - core, 1, keepdims=False)
    far = lax.ppermute(away, "core", [(0, 1), (1, 0)])
    partial, filterbank = dedisperse(delays, core, near, far)
    filterbank = filterbank.reshape(beam_count * owned, -1, FR)
    pieces = partial.reshape(subband_count, TRIALS // subband_count, *partial.shape[1:])
    series = sum_pieces(lax.all_to_all(pieces, sub, 0, 0, tiled=True))
    return (filterbank, series)


def solution(mesh):
    sub, beam = EVERY[:2], EVERY[2:]
    fine = Mesh(mesh.devices.reshape(SIZES), EVERY)
    placed = (
        P(EVERY, None, None, None),
        P(EVERY, None, None, None),
        P(),
        P(sub, None),
    )
    return jax.shard_map(
        on_device,
        mesh=fine,
        in_specs=placed,
        out_specs=(P(sub, beam, None), P(sub, beam, None)),
        check_vma=False,
    )
```

```python
import math

import numpy as np
import jax
import jax.numpy as jnp
from jax import lax
from jax.experimental import pallas as pl
from jax.experimental.pallas import tpu as pltpu
from jax.sharding import Mesh, PartitionSpec as P

A = 1024
NFFT = 1024
C = 256
TRIALS = 32
OUT = 128
FR = 256
HALF = OUT // 2
AXES = (("zh", 2), ("x", 4), ("zl", 2), ("y", 4), ("core", 2))
EVERY = tuple(name for name, size in AXES)
SIZES = tuple(size for name, size in AXES)
ORDER = ("core", "x", "y", "zh", "zl")
TURN = tuple(EVERY.index(name) for name in ORDER)
CHIPS = np.arange(C // 4).reshape(SIZES[:-1]).transpose(TURN[1:]).reshape(-1).tolist()
ROWS = FR - HALF


def dft_table():
    sample = np.arange(NFFT // 4)
    channel = np.arange(C)
    phase = (channel[:, None] * sample[None, :] % NFFT) * (2.0 * math.pi / NFFT)
    cosine = np.cos(phase) / math.sqrt(NFFT)
    sine = np.sin(phase) / math.sqrt(NFFT)
    real_row = np.concatenate([cosine, sine], axis=1)
    imag_row = np.concatenate([-sine, cosine], axis=1)
    rows = np.stack([real_row, imag_row], axis=0)
    rows = rows.reshape(2, C // 4, 4, NFFT // 2).transpose(2, 0, 1, 3)
    return rows.reshape(4, C // 2, NFFT // 2).astype(jnp.bfloat16)


SPAN = 65
BLOCK = 1024
SUBBLOCK = 512
PAIR = 2


def mix_table():
    turn = np.array([1, -1j, -1, 1j])
    table = np.zeros((4, 2, 2, 16, 16, 4, 2, 2))
    for r in range(4):
        for j in range(4):
            c = turn[r * j % 4]
            for half in range(2):
                for f in range(16):
                    table[r, 0, half, f, f, j, half] = (c.real, -c.imag)
                    table[r, 1, half, f, f, j, half] = (c.imag, c.real)
    return table.reshape(256, 256).astype(jnp.bfloat16)


def mix_frames(mix_ref, sample_ref, mixed_ref, row, p):
    start = row + p * 512
    block = jnp.concatenate([sample_ref[start : start + 256, :], sample_ref[start + 256 : start + 512, :]], axis=1)
    got = jnp.dot(mix_ref[...], block, preferred_element_type=jnp.float32).astype(jnp.bfloat16)
    for k in range(16):
        r, lane = k // 4, k % 4 * 128
        for side in range(2):
            first = p * 32 + side * 16
            mixed_ref[r, first : first + 16, lane : lane + 128] = got[16 * k : 16 * k + 16, side * 128 : side * 128 + 128]


def transform(table_ref, mixed_ref, done_ref, antenna, r):
    groups = C // 4
    got = lax.dot_general(
        table_ref[r],
        mixed_ref[r],
        (((1,), (1,)), ((), ())),
        preferred_element_type=jnp.float32,
    )
    for part in range(2):
        start = r * 16 + part * 8 + antenna
        for side in range(2):
            done_ref[side, pl.ds(start, groups, stride=SPAN), :] = got[
                part * groups : part * groups + groups, side * 128 : side * 128 + 128
            ]


def channel_kernel(table_ref, mix_ref, sample_ref, out_ref, mixed_a, mixed_b, done_ref, stage_ref, sems):
    antenna = pl.program_id(0) * PAIR
    last = PAIR * (pl.num_programs(0) - 1)
    before = jnp.where(antenna == 0, last + 1, antenna - 1)

    @pl.when(antenna == 0)
    def _():
        mixed_b[...] = jnp.zeros(mixed_b.shape, mixed_b.dtype)

    for p in range(8):
        mix_frames(mix_ref, sample_ref, mixed_a, 0, p)
        if p % 2 == 0:
            transform(table_ref, mixed_b, done_ref, before, p // 2)
    for p in range(8):
        mix_frames(mix_ref, sample_ref, mixed_b, FR * 16, p)
        if p % 2 == 0:
            transform(table_ref, mixed_a, done_ref, antenna, p // 2)

    @pl.when(antenna == last)
    def _():
        for r in range(4):
            transform(table_ref, mixed_b, done_ref, antenna + 1, r)
        sends = []
        half = C
        for place, q in enumerate(CHIPS):
            for side in range(2):
                lanes = slice(side * 128, side * 128 + 128)
                block = done_ref[side, SPAN * q : SPAN * q + 64, :].reshape(8, 8, 128).astype(jnp.bfloat16)
                for core in range(2):
                    start = core * half + 4 * place
                    stage_ref[start : start + 4, :, lanes] = block[4 * core : 4 * core + 4]
            if place % 16 == 15:
                for core in range(2):
                    rows = pl.ds(core * half + 4 * (place - 15), 64)
                    sem = sems.at[core, place // 16]
                    sends.append(pltpu.make_async_copy(stage_ref.at[rows], out_ref.at[rows], sem))
                    sends[-1].start()
        for send in sends:
            send.wait()


def channelize(voltages):
    antennas = voltages.shape[0]
    rows = FR * 16
    flat = voltages.reshape(antennas, FR, 2, 8, 128).transpose(0, 1, 3, 2, 4).reshape(antennas * rows, 128)
    flat = pltpu.with_memory_space_constraint(flat, pltpu.HBM)
    table = pltpu.with_memory_space_constraint(jnp.asarray(dft_table()), pltpu.HBM)
    mix = pltpu.with_memory_space_constraint(jnp.asarray(mix_table()), pltpu.HBM)
    mixed = pltpu.VMEM((4, FR, NFFT // 2), jnp.bfloat16)
    return pl.pallas_call(
        channel_kernel,
        grid=(antennas // PAIR,),
        in_specs=[
            pl.BlockSpec(table.shape, lambda a: (0, 0, 0)),
            pl.BlockSpec(mix.shape, lambda a: (0, 0)),
            pl.BlockSpec((PAIR * rows, 128), lambda a: (a, 0)),
        ],
        out_specs=pl.BlockSpec(memory_space=pltpu.HBM),
        out_shape=pltpu.HBM((2 * C, antennas, FR), jnp.bfloat16),
        scratch_shapes=[
            mixed,
            mixed,
            pltpu.VMEM((2, C // 4 * SPAN, 128), jnp.float32),
            pltpu.VMEM((2 * C, antennas, FR), jnp.bfloat16),
            pltpu.SemaphoreType.DMA((2, 4)),
        ],
        compiler_params=pltpu.CompilerParams(vmem_limit_bytes=32 << 20),
    )(table, mix, flat)


def beam_kernel(spectra_ref, weight_ref, power_ref, data_ref):
    channel = pl.program_id(0)

    @pl.when(pl.program_id(1) == 0)
    def _():
        for part in range(2):
            data_ref[:, part * FR : (part + 1) * FR] = spectra_ref[:, 2 * channel + part].reshape(A, FR)

    block = SUBBLOCK
    width = power_ref.shape[2]
    for first in range(0, weight_ref.shape[2], block):
        both = weight_ref[0, :, first : first + block].reshape(2 * block, A)
        made = jnp.dot(both, data_ref[...], preferred_element_type=jnp.float32)
        beam_re = made[:block, :FR] - made[block:, FR:]
        beam_im = made[:block, FR:] + made[block:, :FR]
        power = (beam_re * beam_re + beam_im * beam_im).astype(jnp.bfloat16)
        place = (pl.program_id(1) * weight_ref.shape[2] + first) // width
        power_ref[pl.ds(place, block // width), channel] = power.reshape(block // width, width, FR)


def order_kernel(map_ref, weight_ref, out_ref, place_ref):
    @pl.when((pl.program_id(0) == 0) & (pl.program_id(1) == 0))
    def _():
        rows = lax.broadcasted_iota(jnp.int32, (A, A), 0)
        place_ref[...] = jnp.where(rows == map_ref[...], 1.0, 0.0).astype(jnp.bfloat16)

    both = weight_ref[0].reshape(-1, A)
    moved = jnp.dot(both, place_ref[...], preferred_element_type=jnp.float32)
    out_ref[0] = moved.astype(jnp.bfloat16).reshape(out_ref.shape[1:])


def order_weights(antenna_map, weights):
    owned, beams = weights.shape[0], weights.shape[2]
    block = 256
    spec = pl.BlockSpec((1, 2, block, A), lambda k, b: (k, 0, b, 0))
    return pl.pallas_call(
        order_kernel,
        grid=(owned, beams // block),
        in_specs=[pl.BlockSpec((1, A), lambda k, b: (0, 0)), spec],
        out_specs=spec,
        out_shape=pltpu.HBM(weights.shape, jnp.bfloat16),
        scratch_shapes=[pltpu.VMEM((A, A), jnp.bfloat16)],
        compiler_params=pltpu.CompilerParams(vmem_limit_bytes=16 << 20),
    )(antenna_map.reshape(1, A), pltpu.with_memory_space_constraint(weights, pltpu.HBM))


def form_beams(spectra, weights, beam_count):
    owned, beams = weights.shape[0], weights.shape[2]
    block = BLOCK
    width = beams // beam_count
    return pl.pallas_call(
        beam_kernel,
        grid=(owned, beams // block),
        in_specs=[
            pl.BlockSpec(memory_space=pltpu.VMEM),
            pl.BlockSpec((1, 2, block, A), lambda k, b: (k, 0, b, 0)),
        ],
        out_specs=pl.BlockSpec(memory_space=pltpu.VMEM),
        out_shape=jax.ShapeDtypeStruct((beam_count, owned, width, FR), jnp.bfloat16),
        scratch_shapes=[pltpu.VMEM((A, 2 * FR), jnp.bfloat16)],
        compiler_params=pltpu.CompilerParams(vmem_limit_bytes=32 << 20),
    )(spectra, pltpu.with_memory_space_constraint(weights, pltpu.HBM))


def dedisperse_kernel(delay_ref, power_ref, out_ref, kept_ref, turned_ref, sem):
    channels, beams = power_ref.shape[:2]
    keep = pltpu.make_async_copy(power_ref, kept_ref, sem)
    keep.start()
    rows = lax.broadcasted_iota(jnp.int32, (ROWS, FR), 0)
    lanes = lax.broadcasted_iota(jnp.int32, (ROWS, FR), 1)
    unit = jnp.where(rows == lanes, 1.0, 0.0).astype(jnp.bfloat16)

    for pair in range(channels // 2):
        parts = []
        for c in range(2):
            power = power_ref[2 * pair + c]
            parts += [power, jnp.concatenate([power[:, HALF:], power[:, :HALF]], axis=1)]
        both = lax.dot_general(
            unit,
            jnp.concatenate(parts, axis=0),
            (((1,), (1,)), ((), ())),
            preferred_element_type=jnp.float32,
        )
        for c in range(2):
            start = (2 * pair + c) * ROWS
            turned_ref[start : start + ROWS, :] = both[:, c * 2 * beams : (c + 1) * 2 * beams]

    def trial(pair, carry):
        for t in (2 * pair, 2 * pair + 1):
            total = turned_ref[pl.ds(delay_ref[0, t], HALF), :]
            for c in range(1, channels):
                total = total + turned_ref[pl.ds(c * ROWS + delay_ref[c, t], HALF), :]
            out_ref[t] = (total * (1.0 / C)).astype(jnp.bfloat16)
        return carry

    lax.fori_loop(0, TRIALS // 2, trial, 0)
    keep.wait()


def dedisperse(filterbank, delays):
    channels, beams = filterbank.shape[:2]
    return pl.pallas_call(
        dedisperse_kernel,
        in_specs=[
            pl.BlockSpec(memory_space=pltpu.SMEM),
            pl.BlockSpec(memory_space=pltpu.VMEM),
        ],
        out_specs=(
            pl.BlockSpec(memory_space=pltpu.VMEM),
            pl.BlockSpec(memory_space=pltpu.HBM),
        ),
        out_shape=(
            jax.ShapeDtypeStruct((TRIALS, HALF, 2 * beams), jnp.bfloat16),
            jax.ShapeDtypeStruct(filterbank.shape, filterbank.dtype),
        ),
        scratch_shapes=[
            pltpu.VMEM((channels * ROWS, 2 * beams), jnp.float32),
            pltpu.SemaphoreType.DMA,
        ],
        compiler_params=pltpu.CompilerParams(vmem_limit_bytes=16 << 20),
    )(delays, filterbank)


def sum_kernel(pieces_ref, out_ref):
    beams = out_ref.shape[1]
    for t in range(out_ref.shape[0]):
        total = pieces_ref[0, t].astype(jnp.float32)
        for s in range(1, pieces_ref.shape[0]):
            total = total + pieces_ref[s, t].astype(jnp.float32)
        turned = total.T
        out_ref[t] = jnp.concatenate([turned[:beams], turned[beams:]], axis=1)


def sum_pieces(pieces):
    beams = pieces.shape[3] // 2
    return pl.pallas_call(
        sum_kernel,
        out_shape=jax.ShapeDtypeStruct((pieces.shape[1], beams, OUT), jnp.float32),
    )(pieces)


def on_device(voltages, weights, antenna_map, delays):
    sub, beam = EVERY[:2], EVERY[2:]
    subband_count, beam_count = lax.axis_size(sub), lax.axis_size(beam)
    owned = weights.shape[0]
    spectra = channelize(voltages)
    spectra = spectra.reshape(-1, owned * 2, voltages.shape[0], FR)
    moved = lax.all_to_all(spectra, ORDER, 0, 0, tiled=True)
    arrived = antenna_map.reshape(*SIZES, -1).transpose(*TURN, len(SIZES)).reshape(A)
    ordered = order_weights(arrived, weights)
    power = form_beams(moved, ordered, beam_count)
    filterbank = lax.all_to_all(power, beam, 0, 0, tiled=True)
    filterbank = filterbank.reshape(beam_count * owned, -1, FR)
    partial, filterbank = dedisperse(filterbank, delays)
    pieces = partial.reshape(subband_count, TRIALS // subband_count, *partial.shape[1:])
    series = sum_pieces(lax.all_to_all(pieces, sub, 0, 0, tiled=True))
    return (filterbank, series)


def solution(mesh):
    sub, beam = EVERY[:2], EVERY[2:]
    fine = Mesh(mesh.devices.reshape(SIZES), EVERY)
    placed = (
        P(EVERY, None, None, None),
        P(EVERY, None, None, None),
        P(),
        P(sub, None),
    )
    return jax.shard_map(
        on_device,
        mesh=fine,
        in_specs=placed,
        out_specs=(P(sub, beam, None), P(sub, beam, None)),
        check_vma=False,
    )
```

```python
import math

import numpy as np
import jax
import jax.numpy as jnp
from jax import lax
from jax.experimental import pallas as pl
from jax.experimental.pallas import tpu as pltpu
from jax.sharding import Mesh, PartitionSpec as P

A = 1024
NFFT = 1024
C = 256
TRIALS = 32
OUT = 128
FR = 256
HALF = OUT // 2
AXES = (("zh", 2), ("x", 4), ("zl", 2), ("y", 4), ("core", 2))
EVERY = tuple(name for name, size in AXES)
SIZES = tuple(size for name, size in AXES)
ORDER = ("core", "x", "y", "zh", "zl")
TURN = tuple(EVERY.index(name) for name in ORDER)
CHIPS = np.arange(C // 4).reshape(SIZES[:-1]).transpose(TURN[1:]).reshape(-1).tolist()
ROWS = FR - HALF


def dft_table():
    sample = np.arange(NFFT // 4)
    channel = np.arange(C)
    phase = (channel[:, None] * sample[None, :] % NFFT) * (2.0 * math.pi / NFFT)
    cosine = np.cos(phase) / math.sqrt(NFFT)
    sine = np.sin(phase) / math.sqrt(NFFT)
    real_row = np.concatenate([cosine, sine], axis=1)
    imag_row = np.concatenate([-sine, cosine], axis=1)
    rows = np.stack([real_row, imag_row], axis=0)
    rows = rows.reshape(2, C // 4, 4, NFFT // 2).transpose(2, 0, 1, 3)
    return rows.reshape(4, C // 2, NFFT // 2).astype(jnp.bfloat16)


SPAN = 65
BLOCK = 1024
SUBBLOCK = 512
PAIR = 2


def mix_table():
    turn = np.array([1, -1j, -1, 1j])
    table = np.zeros((4, 2, 2, 16, 16, 4, 2, 2))
    for r in range(4):
        for j in range(4):
            c = turn[r * j % 4]
            for half in range(2):
                for f in range(16):
                    table[r, 0, half, f, f, j, half] = (c.real, -c.imag)
                    table[r, 1, half, f, f, j, half] = (c.imag, c.real)
    return table.reshape(256, 256).astype(jnp.bfloat16)


def mix_frames(mix_ref, sample_ref, mixed_ref, row, p):
    start = row + p * 1024
    block = jnp.concatenate([sample_ref[start + 256 * n : start + 256 * n + 256, :] for n in range(4)], axis=1)
    got = jnp.dot(mix_ref[...], block, preferred_element_type=jnp.float32).astype(jnp.bfloat16)
    for k in range(16):
        r, lane = k // 4, k % 4 * 128
        for n in range(4):
            first = p * 64 + n * 16
            mixed_ref[r, first : first + 16, lane : lane + 128] = got[16 * k : 16 * k + 16, n * 128 : n * 128 + 128]


def transform(table_ref, mixed_ref, done_ref, antenna, r):
    groups = C // 4
    got = lax.dot_general(
        table_ref[r],
        mixed_ref[r],
        (((1,), (1,)), ((), ())),
        preferred_element_type=jnp.float32,
    )
    for part in range(2):
        start = r * 16 + part * 8 + antenna
        for side in range(2):
            done_ref[side, pl.ds(start, groups, stride=SPAN), :] = got[
                part * groups : part * groups + groups, side * 128 : side * 128 + 128
            ]


def channel_kernel(table_ref, mix_ref, sample_ref, out_ref, mixed_a, mixed_b, done_ref, stage_ref, sems):
    antenna = pl.program_id(0) * PAIR
    last = PAIR * (pl.num_programs(0) - 1)
    before = jnp.where(antenna == 0, last + 1, antenna - 1)

    for p in range(4):
        mix_frames(mix_ref, sample_ref, mixed_a, 0, p)
        transform(table_ref, mixed_b, done_ref, before, p)
    for p in range(4):
        mix_frames(mix_ref, sample_ref, mixed_b, FR * 16, p)
        transform(table_ref, mixed_a, done_ref, antenna, p)

    @pl.when(antenna == last)
    def _():
        for r in range(4):
            transform(table_ref, mixed_b, done_ref, antenna + 1, r)
        sends = []
        half = C
        for place, q in enumerate(CHIPS):
            for side in range(2):
                lanes = slice(side * 128, side * 128 + 128)
                block = done_ref[side, SPAN * q : SPAN * q + 64, :].reshape(8, 8, 128).astype(jnp.bfloat16)
                for core in range(2):
                    start = core * half + 4 * place
                    stage_ref[start : start + 4, :, lanes] = block[4 * core : 4 * core + 4]
            if place % 16 == 15:
                for core in range(2):
                    rows = pl.ds(core * half + 4 * (place - 15), 64)
                    sem = sems.at[core, place // 16]
                    sends.append(pltpu.make_async_copy(stage_ref.at[rows], out_ref.at[rows], sem))
                    sends[-1].start()
        for send in sends:
            send.wait()


def channelize(voltages):
    antennas = voltages.shape[0]
    rows = FR * 16
    flat = voltages.reshape(antennas, FR, 2, 8, 128).transpose(0, 1, 3, 2, 4).reshape(antennas * rows, 128)
    flat = pltpu.with_memory_space_constraint(flat, pltpu.HBM)
    table = pltpu.with_memory_space_constraint(jnp.asarray(dft_table()), pltpu.HBM)
    mix = pltpu.with_memory_space_constraint(jnp.asarray(mix_table()), pltpu.HBM)
    mixed = pltpu.VMEM((4, FR, NFFT // 2), jnp.bfloat16)
    return pl.pallas_call(
        channel_kernel,
        grid=(antennas // PAIR,),
        in_specs=[
            pl.BlockSpec(table.shape, lambda a: (0, 0, 0)),
            pl.BlockSpec(mix.shape, lambda a: (0, 0)),
            pl.BlockSpec((PAIR * rows, 128), lambda a: (a, 0)),
        ],
        out_specs=pl.BlockSpec(memory_space=pltpu.HBM),
        out_shape=pltpu.HBM((2 * C, antennas, FR), jnp.bfloat16),
        scratch_shapes=[
            mixed,
            mixed,
            pltpu.VMEM((2, C // 4 * SPAN, 128), jnp.float32),
            pltpu.VMEM((2 * C, antennas, FR), jnp.bfloat16),
            pltpu.SemaphoreType.DMA((2, 4)),
        ],
        compiler_params=pltpu.CompilerParams(vmem_limit_bytes=32 << 20),
    )(table, mix, flat)


def beam_kernel(spectra_ref, weight_ref, power_ref, data_ref):
    channel = pl.program_id(0)

    @pl.when(pl.program_id(1) == 0)
    def _():
        for part in range(2):
            data_ref[:, part * FR : (part + 1) * FR] = spectra_ref[:, 2 * channel + part].reshape(A, FR)

    block = SUBBLOCK
    width = power_ref.shape[2]
    for first in range(0, weight_ref.shape[2], block):
        both = weight_ref[0, :, first : first + block].reshape(2 * block, A)
        made = jnp.dot(both, data_ref[...], preferred_element_type=jnp.float32)
        beam_re = made[:block, :FR] - made[block:, FR:]
        beam_im = made[:block, FR:] + made[block:, :FR]
        power = (beam_re * beam_re + beam_im * beam_im).astype(jnp.bfloat16)
        place = (pl.program_id(1) * weight_ref.shape[2] + first) // width
        power_ref[pl.ds(place, block // width), channel] = power.reshape(block // width, width, FR)


def order_kernel(map_ref, weight_ref, out_ref, place_ref):
    @pl.when((pl.program_id(0) == 0) & (pl.program_id(1) == 0))
    def _():
        rows = lax.broadcasted_iota(jnp.int32, (A, A), 0)
        place_ref[...] = jnp.where(rows == map_ref[...], 1.0, 0.0).astype(jnp.bfloat16)

    both = weight_ref[0].reshape(-1, A)
    moved = jnp.dot(both, place_ref[...], preferred_element_type=jnp.float32)
    out_ref[0] = moved.astype(jnp.bfloat16).reshape(out_ref.shape[1:])


def order_weights(antenna_map, weights):
    owned, beams = weights.shape[0], weights.shape[2]
    block = 256
    spec = pl.BlockSpec((1, 2, block, A), lambda k, b: (k, 0, b, 0))
    return pl.pallas_call(
        order_kernel,
        grid=(owned, beams // block),
        in_specs=[pl.BlockSpec((1, A), lambda k, b: (0, 0)), spec],
        out_specs=spec,
        out_shape=pltpu.HBM(weights.shape, jnp.bfloat16),
        scratch_shapes=[pltpu.VMEM((A, A), jnp.bfloat16)],
        compiler_params=pltpu.CompilerParams(vmem_limit_bytes=16 << 20),
    )(antenna_map.reshape(1, A), pltpu.with_memory_space_constraint(weights, pltpu.HBM))


def form_beams(spectra, weights, beam_count):
    owned, beams = weights.shape[0], weights.shape[2]
    block = BLOCK
    width = beams // beam_count
    return pl.pallas_call(
        beam_kernel,
        grid=(owned, beams // block),
        in_specs=[
            pl.BlockSpec(memory_space=pltpu.VMEM),
            pl.BlockSpec((1, 2, block, A), lambda k, b: (k, 0, b, 0)),
        ],
        out_specs=pl.BlockSpec(memory_space=pltpu.VMEM),
        out_shape=jax.ShapeDtypeStruct((beam_count, owned, width, FR), jnp.bfloat16),
        scratch_shapes=[pltpu.VMEM((A, 2 * FR), jnp.bfloat16)],
        compiler_params=pltpu.CompilerParams(vmem_limit_bytes=32 << 20),
    )(spectra, pltpu.with_memory_space_constraint(weights, pltpu.HBM))


def dedisperse_kernel(delay_ref, power_ref, out_ref, kept_ref, turned_ref, sem):
    channels, beams = power_ref.shape[:2]
    keep = pltpu.make_async_copy(power_ref, kept_ref, sem)
    keep.start()
    rows = lax.broadcasted_iota(jnp.int32, (ROWS, FR), 0)
    lanes = lax.broadcasted_iota(jnp.int32, (ROWS, FR), 1)
    unit = jnp.where(rows == lanes, 1.0, 0.0).astype(jnp.bfloat16)

    for pair in range(channels // 2):
        parts = []
        for c in range(2):
            power = power_ref[2 * pair + c]
            parts += [power, jnp.concatenate([power[:, HALF:], power[:, :HALF]], axis=1)]
        both = lax.dot_general(
            unit,
            jnp.concatenate(parts, axis=0),
            (((1,), (1,)), ((), ())),
            preferred_element_type=jnp.float32,
        )
        for c in range(2):
            start = (2 * pair + c) * ROWS
            turned_ref[start : start + ROWS, :] = both[:, c * 2 * beams : (c + 1) * 2 * beams]

    def trial(pair, carry):
        for t in (2 * pair, 2 * pair + 1):
            total = turned_ref[pl.ds(delay_ref[0, t], HALF), :]
            for c in range(1, channels):
                total = total + turned_ref[pl.ds(c * ROWS + delay_ref[c, t], HALF), :]
            out_ref[t] = (total * (1.0 / C)).astype(jnp.bfloat16)
        return carry

    lax.fori_loop(0, TRIALS // 2, trial, 0)
    keep.wait()


def dedisperse(filterbank, delays):
    channels, beams = filterbank.shape[:2]
    return pl.pallas_call(
        dedisperse_kernel,
        in_specs=[
            pl.BlockSpec(memory_space=pltpu.SMEM),
            pl.BlockSpec(memory_space=pltpu.VMEM),
        ],
        out_specs=(
            pl.BlockSpec(memory_space=pltpu.VMEM),
            pl.BlockSpec(memory_space=pltpu.HBM),
        ),
        out_shape=(
            jax.ShapeDtypeStruct((TRIALS, HALF, 2 * beams), jnp.bfloat16),
            jax.ShapeDtypeStruct(filterbank.shape, filterbank.dtype),
        ),
        scratch_shapes=[
            pltpu.VMEM((channels * ROWS, 2 * beams), jnp.float32),
            pltpu.SemaphoreType.DMA,
        ],
        compiler_params=pltpu.CompilerParams(vmem_limit_bytes=16 << 20),
    )(delays, filterbank)


def sum_kernel(pieces_ref, out_ref):
    beams = out_ref.shape[1]
    for t in range(out_ref.shape[0]):
        total = pieces_ref[0, t].astype(jnp.float32)
        for s in range(1, pieces_ref.shape[0]):
            total = total + pieces_ref[s, t].astype(jnp.float32)
        turned = total.T
        out_ref[t] = jnp.concatenate([turned[:beams], turned[beams:]], axis=1)


def sum_pieces(pieces):
    beams = pieces.shape[3] // 2
    return pl.pallas_call(
        sum_kernel,
        in_specs=[pl.BlockSpec(memory_space=pltpu.VMEM)],
        out_specs=pl.BlockSpec(memory_space=pltpu.VMEM),
        out_shape=jax.ShapeDtypeStruct((pieces.shape[1], beams, OUT), jnp.float32),
    )(pltpu.with_memory_space_constraint(pieces, pltpu.VMEM))


def on_device(voltages, weights, antenna_map, delays):
    sub, beam = EVERY[:2], EVERY[2:]
    subband_count, beam_count = lax.axis_size(sub), lax.axis_size(beam)
    owned = weights.shape[0]
    spectra = channelize(voltages)
    spectra = spectra.reshape(-1, owned * 2, voltages.shape[0], FR)
    moved = lax.all_to_all(spectra, ORDER, 0, 0, tiled=True)
    arrived = antenna_map.reshape(*SIZES, -1).transpose(*TURN, len(SIZES)).reshape(A)
    ordered = order_weights(arrived, weights)
    power = form_beams(moved, ordered, beam_count)
    filterbank = lax.all_to_all(power, beam, 0, 0, tiled=True)
    filterbank = filterbank.reshape(beam_count * owned, -1, FR)
    partial, filterbank = dedisperse(filterbank, delays)
    pieces = partial.reshape(subband_count, TRIALS // subband_count, *partial.shape[1:])
    series = sum_pieces(lax.all_to_all(pieces, sub, 0, 0, tiled=True))
    return (filterbank, series)


def solution(mesh):
    sub, beam = EVERY[:2], EVERY[2:]
    fine = Mesh(mesh.devices.reshape(SIZES), EVERY)
    placed = (
        P(EVERY, None, None, None),
        P(EVERY, None, None, None),
        P(),
        P(sub, None),
    )
    return jax.shard_map(
        on_device,
        mesh=fine,
        in_specs=placed,
        out_specs=(P(sub, beam, None), P(sub, beam, None)),
        check_vma=False,
    )
```

```python
import math

import numpy as np
import jax
import jax.numpy as jnp
from jax import lax
from jax.experimental import pallas as pl
from jax.experimental.pallas import tpu as pltpu
from jax.sharding import Mesh, PartitionSpec as P

A = 1024
NFFT = 1024
C = 256
TRIALS = 32
OUT = 128
FR = 256
HALF = OUT // 2
AXES = (("zh", 2), ("x", 4), ("zl", 2), ("y", 4), ("core", 2))
EVERY = tuple(name for name, size in AXES)
SIZES = tuple(size for name, size in AXES)
ORDER = ("core", "x", "y", "zh", "zl")
TURN = tuple(EVERY.index(name) for name in ORDER)
CHIPS = np.arange(C // 4).reshape(SIZES[:-1]).transpose(TURN[1:]).reshape(-1).tolist()
ROWS = FR - HALF


def dft_table():
    sample = np.arange(NFFT // 4)
    channel = np.arange(C)
    phase = (channel[:, None] * sample[None, :] % NFFT) * (2.0 * math.pi / NFFT)
    cosine = np.cos(phase) / math.sqrt(NFFT)
    sine = np.sin(phase) / math.sqrt(NFFT)
    real_row = np.concatenate([cosine, sine], axis=1)
    imag_row = np.concatenate([-sine, cosine], axis=1)
    rows = np.stack([real_row, imag_row], axis=0)
    rows = rows.reshape(2, C // 4, 4, NFFT // 2).transpose(2, 0, 1, 3)
    return rows.reshape(4, C // 2, NFFT // 2).astype(jnp.bfloat16)


SPAN = 65
BLOCK = 1024
SUBBLOCK = 512
PAIR = 2


def mix_table():
    turn = np.array([1, -1j, -1, 1j])
    table = np.zeros((4, 2, 2, 16, 16, 4, 2, 2))
    for r in range(4):
        for j in range(4):
            c = turn[r * j % 4]
            for half in range(2):
                for f in range(16):
                    table[r, 0, half, f, f, j, half] = (c.real, -c.imag)
                    table[r, 1, half, f, f, j, half] = (c.imag, c.real)
    return table.reshape(256, 256).astype(jnp.bfloat16)


def mix_frames(mix_ref, sample_ref, mixed_ref, row, p):
    start = row + p * 1024
    block = jnp.concatenate([sample_ref[start + 256 * n : start + 256 * n + 256, :] for n in range(4)], axis=1)
    got = jnp.dot(mix_ref[...], block, preferred_element_type=jnp.float32).astype(jnp.bfloat16)
    for k in range(16):
        r, lane = k // 4, k % 4 * 128
        for n in range(4):
            first = p * 64 + n * 16
            mixed_ref[r, first : first + 16, lane : lane + 128] = got[16 * k : 16 * k + 16, n * 128 : n * 128 + 128]


def transform(table_ref, mixed_ref, done_ref, antenna, r):
    groups = C // 4
    got = lax.dot_general(
        table_ref[r],
        mixed_ref[r],
        (((1,), (1,)), ((), ())),
        preferred_element_type=jnp.float32,
    )
    for part in range(2):
        start = r * 16 + part * 8 + antenna
        for side in range(2):
            done_ref[side, pl.ds(start, groups, stride=SPAN), :] = got[
                part * groups : part * groups + groups, side * 128 : side * 128 + 128
            ]


def channel_kernel(table_ref, mix_ref, sample_ref, out_ref, mixed_a, mixed_b, done_ref, stage_ref, sems):
    antenna = pl.program_id(0) * PAIR
    last = PAIR * (pl.num_programs(0) - 1)
    before = jnp.where(antenna == 0, last + 1, antenna - 1)

    for p in range(4):
        mix_frames(mix_ref, sample_ref, mixed_a, 0, p)
        transform(table_ref, mixed_b, done_ref, before, p)
    for p in range(4):
        mix_frames(mix_ref, sample_ref, mixed_b, FR * 16, p)
        transform(table_ref, mixed_a, done_ref, antenna, p)

    @pl.when(antenna == last)
    def _():
        for r in range(4):
            transform(table_ref, mixed_b, done_ref, antenna + 1, r)
        sends = []
        half = C
        for place, q in enumerate(CHIPS):
            for side in range(2):
                lanes = slice(side * 128, side * 128 + 128)
                block = done_ref[side, SPAN * q : SPAN * q + 64, :].reshape(8, 8, 128).astype(jnp.bfloat16)
                for core in range(2):
                    start = core * half + 4 * place
                    stage_ref[start : start + 4, :, lanes] = block[4 * core : 4 * core + 4]
            if place % 16 == 15:
                for core in range(2):
                    rows = pl.ds(core * half + 4 * (place - 15), 64)
                    sem = sems.at[core, place // 16]
                    sends.append(pltpu.make_async_copy(stage_ref.at[rows], out_ref.at[rows], sem))
                    sends[-1].start()
        for send in sends:
            send.wait()


def channelize(voltages):
    antennas = voltages.shape[0]
    rows = FR * 16
    flat = voltages.reshape(antennas, FR, 2, 8, 128).transpose(0, 1, 3, 2, 4).reshape(antennas * rows, 128)
    flat = pltpu.with_memory_space_constraint(flat, pltpu.HBM)
    table = pltpu.with_memory_space_constraint(jnp.asarray(dft_table()), pltpu.HBM)
    mix = pltpu.with_memory_space_constraint(jnp.asarray(mix_table()), pltpu.HBM)
    mixed = pltpu.VMEM((4, FR, NFFT // 2), jnp.bfloat16)
    return pl.pallas_call(
        channel_kernel,
        grid=(antennas // PAIR,),
        in_specs=[
            pl.BlockSpec(table.shape, lambda a: (0, 0, 0)),
            pl.BlockSpec(mix.shape, lambda a: (0, 0)),
            pl.BlockSpec((PAIR * rows, 128), lambda a: (a, 0)),
        ],
        out_specs=pl.BlockSpec(memory_space=pltpu.HBM),
        out_shape=pltpu.HBM((2 * C, antennas, FR), jnp.bfloat16),
        scratch_shapes=[
            mixed,
            mixed,
            pltpu.VMEM((2, C // 4 * SPAN, 128), jnp.float32),
            pltpu.VMEM((2 * C, antennas, FR), jnp.bfloat16),
            pltpu.SemaphoreType.DMA((2, 4)),
        ],
        compiler_params=pltpu.CompilerParams(vmem_limit_bytes=32 << 20),
    )(table, mix, flat)


def beam_kernel(spectra_ref, weight_ref, power_ref, data_ref):
    channel = pl.program_id(0)

    @pl.when(pl.program_id(1) == 0)
    def _():
        for part in range(2):
            data_ref[:, part * FR : (part + 1) * FR] = spectra_ref[:, 2 * channel + part].reshape(A, FR)

    block = SUBBLOCK
    width = power_ref.shape[2]
    for first in range(0, weight_ref.shape[2], block):
        both = weight_ref[0, :, first : first + block].reshape(2 * block, A)
        made = jnp.dot(both, data_ref[...], preferred_element_type=jnp.float32)
        beam_re = made[:block, :FR] - made[block:, FR:]
        beam_im = made[:block, FR:] + made[block:, :FR]
        power = (beam_re * beam_re + beam_im * beam_im).astype(jnp.bfloat16)
        place = (pl.program_id(1) * weight_ref.shape[2] + first) // width
        power_ref[pl.ds(place, block // width), channel] = power.reshape(block // width, width, FR)


def order_kernel(map_ref, weight_ref, out_ref, place_ref):
    @pl.when((pl.program_id(0) == 0) & (pl.program_id(1) == 0))
    def _():
        rows = lax.broadcasted_iota(jnp.int32, (A, A), 0)
        place_ref[...] = jnp.where(rows == map_ref[...], 1.0, 0.0).astype(jnp.bfloat16)

    both = weight_ref[0].reshape(-1, A)
    moved = jnp.dot(both, place_ref[...], preferred_element_type=jnp.float32)
    out_ref[0] = moved.astype(jnp.bfloat16).reshape(out_ref.shape[1:])


def order_weights(antenna_map, weights):
    owned, beams = weights.shape[0], weights.shape[2]
    block = 256
    spec = pl.BlockSpec((1, 2, block, A), lambda k, b: (k, 0, b, 0))
    return pl.pallas_call(
        order_kernel,
        grid=(owned, beams // block),
        in_specs=[pl.BlockSpec((1, A), lambda k, b: (0, 0)), spec],
        out_specs=spec,
        out_shape=pltpu.HBM(weights.shape, jnp.bfloat16),
        scratch_shapes=[pltpu.VMEM((A, A), jnp.bfloat16)],
        compiler_params=pltpu.CompilerParams(vmem_limit_bytes=16 << 20),
    )(antenna_map.reshape(1, A), pltpu.with_memory_space_constraint(weights, pltpu.HBM))


def form_beams(spectra, weights, beam_count):
    owned, beams = weights.shape[0], weights.shape[2]
    block = BLOCK
    width = beams // beam_count
    return pl.pallas_call(
        beam_kernel,
        grid=(owned, beams // block),
        in_specs=[
            pl.BlockSpec(memory_space=pltpu.VMEM),
            pl.BlockSpec((1, 2, block, A), lambda k, b: (k, 0, b, 0)),
        ],
        out_specs=pl.BlockSpec(memory_space=pltpu.VMEM),
        out_shape=jax.ShapeDtypeStruct((beam_count, owned, width, FR), jnp.bfloat16),
        scratch_shapes=[pltpu.VMEM((A, 2 * FR), jnp.bfloat16)],
        compiler_params=pltpu.CompilerParams(vmem_limit_bytes=32 << 20),
    )(spectra, pltpu.with_memory_space_constraint(weights, pltpu.HBM))


def dedisperse_kernel(delay_ref, core_ref, near_ref, far_ref, out_ref, kept_ref, turned_ref, sems):
    chips, _, owned, beams = near_ref.shape[:4]
    channels = chips * 2 * owned
    core = core_ref[0]
    copies = [
        pltpu.make_async_copy(near_ref.at[:, core], kept_ref.at[:, core], sems.at[0]),
        pltpu.make_async_copy(far_ref, kept_ref.at[:, 1 - core], sems.at[1]),
    ]
    for copy in copies:
        copy.start()
    rows = lax.broadcasted_iota(jnp.int32, (ROWS, FR), 0)
    lanes = lax.broadcasted_iota(jnp.int32, (ROWS, FR), 1)
    unit = jnp.where(rows == lanes, 1.0, 0.0).astype(jnp.bfloat16)

    for chip in range(chips):
        for side in range(2):
            parts = []
            for k in range(owned):
                power = near_ref[chip, core, k] if side == 0 else far_ref[chip, k]
                parts += [power, jnp.concatenate([power[:, HALF:], power[:, :HALF]], axis=1)]
            both = lax.dot_general(
                unit,
                jnp.concatenate(parts, axis=0),
                (((1,), (1,)), ((), ())),
                preferred_element_type=jnp.float32,
            )
            source = core if side == 0 else 1 - core
            for k in range(owned):
                start = pl.multiple_of(((chip * 2 + source) * owned + k) * ROWS, 8)
                turned_ref[pl.ds(start, ROWS), :] = both[:, k * 2 * beams : (k + 1) * 2 * beams]

    def trial(pair, carry):
        for t in (2 * pair, 2 * pair + 1):
            total = turned_ref[pl.ds(delay_ref[0, t], HALF), :]
            for c in range(1, channels):
                total = total + turned_ref[pl.ds(c * ROWS + delay_ref[c, t], HALF), :]
            out_ref[t] = (total * (1.0 / C)).astype(jnp.bfloat16)
        return carry

    lax.fori_loop(0, TRIALS // 2, trial, 0)
    for copy in copies:
        copy.wait()


def dedisperse(delays, core, near, far):
    chips, _, owned, beams = near.shape[:4]
    channels = chips * 2 * owned
    return pl.pallas_call(
        dedisperse_kernel,
        in_specs=[
            pl.BlockSpec(memory_space=pltpu.SMEM),
            pl.BlockSpec(memory_space=pltpu.SMEM),
            pl.BlockSpec(memory_space=pltpu.VMEM),
            pl.BlockSpec(memory_space=pltpu.VMEM),
        ],
        out_specs=(
            pl.BlockSpec(memory_space=pltpu.VMEM),
            pl.BlockSpec(memory_space=pltpu.HBM),
        ),
        out_shape=(
            jax.ShapeDtypeStruct((TRIALS, HALF, 2 * beams), jnp.bfloat16),
            jax.ShapeDtypeStruct(near.shape, near.dtype),
        ),
        scratch_shapes=[
            pltpu.VMEM((channels * ROWS, 2 * beams), jnp.float32),
            pltpu.SemaphoreType.DMA((2,)),
        ],
        compiler_params=pltpu.CompilerParams(vmem_limit_bytes=16 << 20),
    )(delays, core.reshape(1), near, far)


def sum_kernel(pieces_ref, out_ref):
    beams = out_ref.shape[1]
    for t in range(out_ref.shape[0]):
        total = pieces_ref[0, t].astype(jnp.float32)
        for s in range(1, pieces_ref.shape[0]):
            total = total + pieces_ref[s, t].astype(jnp.float32)
        turned = total.T
        out_ref[t] = jnp.concatenate([turned[:beams], turned[beams:]], axis=1)


def sum_pieces(pieces):
    beams = pieces.shape[3] // 2
    return pl.pallas_call(
        sum_kernel,
        in_specs=[pl.BlockSpec(memory_space=pltpu.VMEM)],
        out_specs=pl.BlockSpec(memory_space=pltpu.VMEM),
        out_shape=jax.ShapeDtypeStruct((pieces.shape[1], beams, OUT), jnp.float32),
    )(pltpu.with_memory_space_constraint(pieces, pltpu.VMEM))


def on_device(voltages, weights, antenna_map, delays):
    sub, beam = EVERY[:2], EVERY[2:]
    subband_count, beam_count = lax.axis_size(sub), lax.axis_size(beam)
    owned = weights.shape[0]
    spectra = channelize(voltages)
    spectra = spectra.reshape(-1, owned * 2, voltages.shape[0], FR)
    core = lax.axis_index("core")
    spectra, core, delays = lax.optimization_barrier((spectra, core, delays))
    moved = lax.all_to_all(spectra, ORDER, 0, 0, tiled=True)
    arrived = antenna_map.reshape(*SIZES, -1).transpose(*TURN, len(SIZES)).reshape(A)
    ordered = order_weights(arrived, weights)
    power = form_beams(moved, ordered, beam_count)
    power = power.reshape(beam_count // 2, 2, *power.shape[1:])
    near = lax.all_to_all(power, ("zl", "y"), 0, 0, tiled=True)
    near, core = lax.optimization_barrier((near, core))
    away = lax.dynamic_index_in_dim(near, 1 - core, 1, keepdims=False)
    far = lax.ppermute(away, "core", [(0, 1), (1, 0)])
    partial, filterbank = dedisperse(delays, core, near, far)
    filterbank = filterbank.reshape(beam_count * owned, -1, FR)
    pieces = partial.reshape(subband_count, TRIALS // subband_count, *partial.shape[1:])
    series = sum_pieces(lax.all_to_all(pieces, sub, 0, 0, tiled=True))
    return (filterbank, series)


def solution(mesh):
    sub, beam = EVERY[:2], EVERY[2:]
    fine = Mesh(mesh.devices.reshape(SIZES), EVERY)
    placed = (
        P(EVERY, None, None, None),
        P(EVERY, None, None, None),
        P(),
        P(sub, None),
    )
    return jax.shard_map(
        on_device,
        mesh=fine,
        in_specs=placed,
        out_specs=(P(sub, beam, None), P(sub, beam, None)),
        check_vma=False,
    )
```

```python
import math

import numpy as np
import jax
import jax.numpy as jnp
from jax import lax
from jax.experimental import pallas as pl
from jax.experimental.pallas import tpu as pltpu
from jax.sharding import Mesh, PartitionSpec as P

A = 1024
NFFT = 1024
C = 256
TRIALS = 32
OUT = 128
FR = 256
HALF = OUT // 2
AXES = (("zh", 2), ("x", 4), ("zl", 2), ("y", 4), ("core", 2))
EVERY = tuple(name for name, size in AXES)
SIZES = tuple(size for name, size in AXES)
ORDER = ("core", "x", "y", "zh", "zl")
TURN = tuple(EVERY.index(name) for name in ORDER)
CHIPS = np.arange(C // 4).reshape(SIZES[:-1]).transpose(TURN[1:]).reshape(-1).tolist()
ROWS = FR - HALF


def dft_table():
    sample = np.arange(NFFT // 4)
    channel = np.arange(C)
    phase = (channel[:, None] * sample[None, :] % NFFT) * (2.0 * math.pi / NFFT)
    cosine = np.cos(phase) / math.sqrt(NFFT)
    sine = np.sin(phase) / math.sqrt(NFFT)
    real_row = np.concatenate([cosine, sine], axis=1)
    imag_row = np.concatenate([-sine, cosine], axis=1)
    rows = np.stack([real_row, imag_row], axis=0)
    rows = rows.reshape(2, C // 4, 4, NFFT // 2).transpose(2, 0, 1, 3)
    return rows.reshape(4, C // 2, NFFT // 2).astype(jnp.bfloat16)


SPAN = 65
SUBB = 256
PARTS = 2
PAIR = 2


def mix_table():
    turn = np.array([1, -1j, -1, 1j])
    table = np.zeros((4, 2, 2, 16, 16, 4, 2, 2))
    for r in range(4):
        for j in range(4):
            c = turn[r * j % 4]
            for half in range(2):
                for f in range(16):
                    table[r, 0, half, f, f, j, half] = (c.real, -c.imag)
                    table[r, 1, half, f, f, j, half] = (c.imag, c.real)
    return table.reshape(256, 256).astype(jnp.bfloat16)


def mix_frames(mix_ref, sample_ref, mixed_ref, row, p):
    start = row + p * 1024
    block = jnp.concatenate([sample_ref[start + 256 * n : start + 256 * n + 256, :] for n in range(4)], axis=1)
    got = jnp.dot(mix_ref[...], block, preferred_element_type=jnp.float32).astype(jnp.bfloat16)
    for k in range(16):
        r, lane = k // 4, k % 4 * 128
        for n in range(4):
            first = p * 64 + n * 16
            mixed_ref[r, first : first + 16, lane : lane + 128] = got[16 * k : 16 * k + 16, n * 128 : n * 128 + 128]


def transform(table_ref, mixed_ref, done_ref, antenna, r):
    groups = C // 4
    got = lax.dot_general(
        table_ref[r],
        mixed_ref[r],
        (((1,), (1,)), ((), ())),
        preferred_element_type=jnp.float32,
    )
    for part in range(2):
        start = r * 16 + part * 8 + antenna
        for side in range(2):
            done_ref[side, pl.ds(start, groups, stride=SPAN), :] = got[
                part * groups : part * groups + groups, side * 128 : side * 128 + 128
            ]


def channel_kernel(table_ref, mix_ref, sample_ref, out_ref, mixed_a, mixed_b, done_ref, stage_ref, sems):
    antenna = pl.program_id(0) * PAIR
    last = PAIR * (pl.num_programs(0) - 1)
    before = jnp.where(antenna == 0, last + 1, antenna - 1)

    for p in range(4):
        mix_frames(mix_ref, sample_ref, mixed_a, 0, p)
        transform(table_ref, mixed_b, done_ref, before, p)
    for p in range(4):
        mix_frames(mix_ref, sample_ref, mixed_b, FR * 16, p)
        transform(table_ref, mixed_a, done_ref, antenna, p)

    @pl.when(antenna == last)
    def _():
        for r in range(4):
            transform(table_ref, mixed_b, done_ref, antenna + 1, r)
        sends = []
        half = C
        for place, q in enumerate(CHIPS):
            for side in range(2):
                lanes = slice(side * 128, side * 128 + 128)
                block = done_ref[side, SPAN * q : SPAN * q + 64, :].reshape(8, 8, 128).astype(jnp.bfloat16)
                for core in range(2):
                    start = core * half + 4 * place
                    stage_ref[start : start + 4, :, lanes] = block[4 * core : 4 * core + 4]
            if place % 16 == 15:
                for core in range(2):
                    rows = pl.ds(core * half + 4 * (place - 15), 64)
                    sem = sems.at[core, place // 16]
                    sends.append(pltpu.make_async_copy(stage_ref.at[rows], out_ref.at[rows], sem))
                    sends[-1].start()
        for send in sends:
            send.wait()


def channelize(voltages):
    antennas = voltages.shape[0]
    rows = FR * 16
    flat = voltages.reshape(antennas, FR, 2, 8, 128).transpose(0, 1, 3, 2, 4).reshape(antennas * rows, 128)
    flat = pltpu.with_memory_space_constraint(flat, pltpu.HBM)
    table = pltpu.with_memory_space_constraint(jnp.asarray(dft_table()), pltpu.HBM)
    mix = pltpu.with_memory_space_constraint(jnp.asarray(mix_table()), pltpu.HBM)
    mixed = pltpu.VMEM((4, FR, NFFT // 2), jnp.bfloat16)
    return pl.pallas_call(
        channel_kernel,
        grid=(antennas // PAIR,),
        in_specs=[
            pl.BlockSpec(table.shape, lambda a: (0, 0, 0)),
            pl.BlockSpec(mix.shape, lambda a: (0, 0)),
            pl.BlockSpec((PAIR * rows, 128), lambda a: (a, 0)),
        ],
        out_specs=pl.BlockSpec(memory_space=pltpu.HBM),
        out_shape=pltpu.HBM((2 * C, antennas, FR), jnp.bfloat16),
        scratch_shapes=[
            mixed,
            mixed,
            pltpu.VMEM((2, C // 4 * SPAN, 128), jnp.float32),
            pltpu.VMEM((2 * C, antennas, FR), jnp.bfloat16),
            pltpu.SemaphoreType.DMA((2, 4)),
        ],
        compiler_params=pltpu.CompilerParams(vmem_limit_bytes=32 << 20),
    )(table, mix, flat)


def beam_kernel(spectra_ref, weight_ref, power_ref, data_ref, held_ref, sems):
    channel = pl.program_id(0)
    parts = held_ref.shape[1]
    size = held_ref.shape[3]

    def fetch(k, n):
        return pltpu.make_async_copy(
            weight_ref.at[k, :, pl.ds(n * size, size), :], held_ref.at[k, n], sems.at[k, n]
        )

    @pl.when(channel == 0)
    def _():
        for k in range(held_ref.shape[0]):
            for n in range(parts):
                fetch(k, n).start()

    for part in range(2):
        data_ref[:, part * FR : (part + 1) * FR] = spectra_ref[:, 2 * channel + part].reshape(A, FR)
    block = SUBB
    width = power_ref.shape[2]
    for n in range(parts):
        fetch(channel, n).wait()
        for first in range(0, size, block):
            both = held_ref[channel, n, :, first : first + block].reshape(2 * block, A)
            made = jnp.dot(both, data_ref[...], preferred_element_type=jnp.float32)
            beam_re = made[:block, :FR] - made[block:, FR:]
            beam_im = made[:block, FR:] + made[block:, :FR]
            power = (beam_re * beam_re + beam_im * beam_im).astype(jnp.bfloat16)
            place = (n * size + first) // width
            power_ref[place : place + block // width, channel] = power.reshape(block // width, width, FR)


def order_kernel(map_ref, weight_ref, out_ref, place_ref):
    @pl.when((pl.program_id(0) == 0) & (pl.program_id(1) == 0))
    def _():
        rows = lax.broadcasted_iota(jnp.int32, (A, A), 0)
        place_ref[...] = jnp.where(rows == map_ref[...], 1.0, 0.0).astype(jnp.bfloat16)

    both = weight_ref[0].reshape(-1, A)
    moved = jnp.dot(both, place_ref[...], preferred_element_type=jnp.float32)
    out_ref[0] = moved.astype(jnp.bfloat16).reshape(out_ref.shape[1:])


def order_weights(antenna_map, weights):
    owned, beams = weights.shape[0], weights.shape[2]
    block = 256
    spec = pl.BlockSpec((1, 2, block, A), lambda k, b: (k, 0, b, 0))
    return pl.pallas_call(
        order_kernel,
        grid=(owned, beams // block),
        in_specs=[pl.BlockSpec((1, A), lambda k, b: (0, 0)), spec],
        out_specs=spec,
        out_shape=pltpu.HBM(weights.shape, jnp.bfloat16),
        scratch_shapes=[pltpu.VMEM((A, A), jnp.bfloat16)],
        compiler_params=pltpu.CompilerParams(vmem_limit_bytes=16 << 20),
    )(antenna_map.reshape(1, A), pltpu.with_memory_space_constraint(weights, pltpu.HBM))


def form_beams(spectra, weights, beam_count):
    owned, beams = weights.shape[0], weights.shape[2]
    width = beams // beam_count
    parts = PARTS
    return pl.pallas_call(
        beam_kernel,
        grid=(owned,),
        in_specs=[
            pl.BlockSpec(memory_space=pltpu.VMEM),
            pl.BlockSpec(memory_space=pltpu.HBM),
        ],
        out_specs=pl.BlockSpec(memory_space=pltpu.VMEM),
        out_shape=jax.ShapeDtypeStruct((beam_count, owned, width, FR), jnp.bfloat16),
        scratch_shapes=[
            pltpu.VMEM((A, 2 * FR), jnp.bfloat16),
            pltpu.VMEM((owned, parts, 2, beams // parts, A), jnp.bfloat16),
            pltpu.SemaphoreType.DMA((owned, parts)),
        ],
        compiler_params=pltpu.CompilerParams(vmem_limit_bytes=32 << 20),
    )(spectra, pltpu.with_memory_space_constraint(weights, pltpu.HBM))


def dedisperse_kernel(delay_ref, power_ref, out_ref, kept_ref, turned_ref, sem):
    channels, beams = power_ref.shape[:2]
    keep = pltpu.make_async_copy(power_ref, kept_ref, sem)
    keep.start()
    rows = lax.broadcasted_iota(jnp.int32, (ROWS, FR), 0)
    lanes = lax.broadcasted_iota(jnp.int32, (ROWS, FR), 1)
    unit = jnp.where(rows == lanes, 1.0, 0.0).astype(jnp.bfloat16)

    for pair in range(channels // 2):
        parts = []
        for c in range(2):
            power = power_ref[2 * pair + c]
            parts += [power, jnp.concatenate([power[:, HALF:], power[:, :HALF]], axis=1)]
        both = lax.dot_general(
            unit,
            jnp.concatenate(parts, axis=0),
            (((1,), (1,)), ((), ())),
            preferred_element_type=jnp.float32,
        )
        for c in range(2):
            start = (2 * pair + c) * ROWS
            turned_ref[start : start + ROWS, :] = both[:, c * 2 * beams : (c + 1) * 2 * beams]

    def trial(pair, carry):
        for t in (2 * pair, 2 * pair + 1):
            total = turned_ref[pl.ds(delay_ref[0, t], HALF), :]
            for c in range(1, channels):
                total = total + turned_ref[pl.ds(c * ROWS + delay_ref[c, t], HALF), :]
            owner = t // 4
            place = (owner % 4 * 2 + owner // 4) * 4 + t % 4
            out_ref[place] = (total * (1.0 / C)).astype(jnp.bfloat16)
        return carry

    lax.fori_loop(0, TRIALS // 2, trial, 0)
    keep.wait()


def dedisperse(filterbank, delays):
    channels, beams = filterbank.shape[:2]
    return pl.pallas_call(
        dedisperse_kernel,
        in_specs=[
            pl.BlockSpec(memory_space=pltpu.SMEM),
            pl.BlockSpec(memory_space=pltpu.VMEM),
        ],
        out_specs=(
            pl.BlockSpec(memory_space=pltpu.VMEM),
            pl.BlockSpec(memory_space=pltpu.HBM),
        ),
        out_shape=(
            jax.ShapeDtypeStruct((TRIALS, HALF, 2 * beams), jnp.bfloat16),
            jax.ShapeDtypeStruct(filterbank.shape, filterbank.dtype),
        ),
        scratch_shapes=[
            pltpu.VMEM((channels * ROWS, 2 * beams), jnp.float32),
            pltpu.SemaphoreType.DMA,
        ],
        compiler_params=pltpu.CompilerParams(
            vmem_limit_bytes=16 << 20
        ),
    )(delays, filterbank)


def sum_kernel(pieces_ref, out_ref):
    beams = out_ref.shape[1]
    for t in range(out_ref.shape[0]):
        total = pieces_ref[0, t].astype(jnp.float32)
        for s in range(1, pieces_ref.shape[0]):
            total = total + pieces_ref[s, t].astype(jnp.float32)
        turned = total.T
        out_ref[t] = jnp.concatenate([turned[:beams], turned[beams:]], axis=1)


def sum_pieces(pieces):
    beams = pieces.shape[3] // 2
    return pl.pallas_call(
        sum_kernel,
        in_specs=[pl.BlockSpec(memory_space=pltpu.VMEM)],
        out_specs=pl.BlockSpec(memory_space=pltpu.VMEM),
        out_shape=jax.ShapeDtypeStruct((pieces.shape[1], beams, OUT), jnp.float32),
    )(pltpu.with_memory_space_constraint(pieces, pltpu.VMEM))


def on_device(voltages, weights, antenna_map, delays):
    sub, beam = EVERY[:2], EVERY[2:]
    subband_count, beam_count = lax.axis_size(sub), lax.axis_size(beam)
    owned = weights.shape[0]
    spectra = channelize(voltages)
    spectra = spectra.reshape(-1, owned * 2, voltages.shape[0], FR)
    moved = lax.all_to_all(spectra, ORDER, 0, 0, tiled=True)
    arrived = antenna_map.reshape(*SIZES, -1).transpose(*TURN, len(SIZES)).reshape(A)
    ordered = order_weights(arrived, weights)
    power = form_beams(moved, ordered, beam_count)
    filterbank = lax.all_to_all(power, beam, 0, 0, tiled=True)
    filterbank = filterbank.reshape(beam_count * owned, -1, FR)
    partial, filterbank = dedisperse(filterbank, delays)
    pieces = partial.reshape(subband_count, TRIALS // subband_count, *partial.shape[1:])
    series = sum_pieces(lax.all_to_all(pieces, sub[::-1], 0, 0, tiled=True))
    return (filterbank, series)


def solution(mesh):
    sub, beam = EVERY[:2], EVERY[2:]
    fine = Mesh(mesh.devices.reshape(SIZES), EVERY)
    placed = (
        P(EVERY, None, None, None),
        P(EVERY, None, None, None),
        P(),
        P(sub, None),
    )
    return jax.shard_map(
        on_device,
        mesh=fine,
        in_specs=placed,
        out_specs=(P(sub, beam, None), P(sub, beam, None)),
        check_vma=False,
    )
```
